32 devices in a mesh: dp: 8 (over y, x, core), seq: 4 (over z).
Axes of the slice: x: 2, y: 2, z: 4, core: 2. Of those that a mesh axis runs over, the one named last changes fastest.
Arguments:
- latents_in: bfloat16 [16, 256, 768], P('dp', 'seq'), may hold values from -6 to 6
- conditioning: bfloat16 [16, 768], P('dp'), may hold values from -4 to 4
- out_cotangent: bfloat16 [16, 256, 768], P('dp', 'seq'), may hold values from -6 to 6
- modulation_weight: bfloat16 [768, 4608], P(('dp', 'seq')), may hold values from -0.21875 to 0.21875
- modulation_bias: bfloat16 [4608], P(('dp', 'seq')), may hold values from -3 to 3
- qkv_weight: bfloat16 [768, 2304], P(('dp', 'seq')), may hold values from -0.21875 to 0.21875
- qv_bias: bfloat16 [1536], P(('dp', 'seq')), may hold values from -3 to 3
- proj_weight: bfloat16 [768, 768], P(('dp', 'seq')), may hold values from -0.875 to 0.875
- proj_bias: bfloat16 [768], P(('dp', 'seq')), may hold values from -2 to 2
- mlp_in_weight: bfloat16 [768, 3072], P(('dp', 'seq')), may hold values from -0.21875 to 0.21875
- mlp_in_bias: bfloat16 [3072], P(('dp', 'seq')), may hold values from -3 to 3
- mlp_out_weight: bfloat16 [3072, 768], P(('dp', 'seq')), may hold values from -0.109375 to 0.109375
- mlp_out_bias: bfloat16 [768], P(('dp', 'seq')), may hold values from -3 to 3
Outputs:
- block_out: float32 [16, 256, 768], P('dp', 'seq')
- grad_latents: float32 [16, 256, 768], P('dp', 'seq')
- grad_conditioning: float32 [16, 768], P('dp')
- grad_modulation_weight: float32 [768, 4608], P(('dp', 'seq'))
- grad_modulation_bias: float32 [4608], P(('dp', 'seq'))
- grad_qkv_weight: float32 [768, 2304], P(('dp', 'seq'))
- grad_qv_bias: float32 [1536], P(('dp', 'seq'))
- grad_proj_weight: float32 [768, 768], P(('dp', 'seq'))
- grad_proj_bias: float32 [768], P(('dp', 'seq'))
- grad_mlp_in_weight: float32 [768, 3072], P(('dp', 'seq'))
- grad_mlp_in_bias: float32 [3072], P(('dp', 'seq'))
- grad_mlp_out_weight: float32 [3072, 768], P(('dp', 'seq'))
- grad_mlp_out_bias: float32 [768], P(('dp', 'seq'))
The draws below stay inside these ranges and needn't reach their ends.
All inputs are finite; a program needn't handle non-finite values.
Results may differ from the reference program's by a relative error of at most 0.012.
The reference program's roundings to bfloat16 on the way count: a program that leaves them out, or rounds other values in their place, can miss the bound.
Values may be sent and summed in bfloat16 or wider, within the bound.
A program may use at most 192 MiB of HBM per device.

```python
import math
import jax
import jax.numpy as jnp
from jax import lax

D = 768
HEADS = 12
FF = 3072
L = 256
LATENTS = 16


def strengthened(array, key, source, target, blocks, factor):
    owner, partner = [(jnp.arange(array.shape[axis_at]) // (array.shape[axis_at] // blocks)).reshape([-1 if axis == axis_at else 1 for axis in range(array.ndim)]) for axis_at in (source, target)]
    chosen = jax.random.permutation(key, blocks)[partner]
    strong = (owner == chosen) | (owner == (partner + blocks // 2) % blocks)
    return jnp.where(strong, factor * array, array)


def steps_of(stream_key, extent, cuts, low, top_value):
    gain = 1.0
    for axis_at, blocks in cuts:
        draws = jax.random.uniform(jax.random.fold_in(jax.random.fold_in(stream_key, 6), axis_at), (blocks,), jnp.float32, low / len(cuts), top_value / len(cuts))
        gain = gain * jnp.repeat(jnp.exp(draws), extent[axis_at] // blocks).reshape((-1,) + (1,) * (len(extent) - 1 - axis_at))
    return gain


def normal_values(rng, dims, spread, limit, cuts=(), held_as=jnp.bfloat16):
    factor_of = steps_of(rng, dims, cuts, -0.22, 0.18) if cuts else 1.0
    array = jax.random.normal(rng, dims, jnp.float32) * spread * factor_of
    return jnp.minimum(jnp.maximum(array, -limit), limit).astype(held_as)


def gaussian_with(stream_key, shape, scale, reach, shards, heavy, kind=jnp.bfloat16):
    drawn = scale * jax.random.normal(stream_key, shape, jnp.float32)
    if shards:
        drawn = drawn * steps_of(stream_key, shape, shards, -0.22, 0.18)
    return jnp.clip(strengthened(drawn, jax.random.fold_in(stream_key, 3), *heavy), -reach, reach).astype(kind)


def setup_inputs(seed: int = 0) -> dict:
    seeds = jax.random.split(jax.random.key(seed), 14)
    latents_in = normal_values(seeds[0], (LATENTS, L, D), 1.0, 6.0, ((0, 8), (1, 4)))
    conditioning = normal_values(seeds[1], (LATENTS, D), 1.0, 4.0, ((0, 8),))
    out_cotangent = gaussian_with(seeds[2], (LATENTS, L, D), 1.0, 6.0, ((0, 8), (1, 4)), (0, 2, 8, 2.0))
    modulation_weight = normal_values(seeds[3], (D, 6 * D), D ** -0.5, 0.21875, ((0, 32),))
    modulation_bias = normal_values(seeds[4], (6 * D,), 0.5, 3.0, ((0, 32),))
    qkv_weight = normal_values(seeds[5], (D, 3 * D), D ** -0.5, 0.21875, ((0, 32),))
    qv_bias = normal_values(seeds[6], (2 * D,), 0.5, 3.0, ((0, 32),))
    proj_weight = normal_values(seeds[7], (D, D), (D // 16) ** -0.5, 0.875, ((0, 32),))
    proj_bias = normal_values(seeds[8], (D,), 0.3, 2.0, ((0, 32),))
    mlp_in_weight = normal_values(seeds[9], (D, FF), D ** -0.5, 0.21875, ((0, 32),))
    mlp_in_bias = normal_values(seeds[10], (FF,), 0.5, 3.0, ((0, 32),))
    mlp_out_weight = normal_values(seeds[11], (FF, D), FF ** -0.5, 0.109375, ((0, 32),))
    mlp_out_bias = normal_values(seeds[12], (D,), 0.5, 3.0, ((0, 32),))
    return {"latents_in": latents_in, "conditioning": conditioning, "out_cotangent": out_cotangent, "modulation_weight": modulation_weight, "modulation_bias": modulation_bias, "qkv_weight": qkv_weight, "qv_bias": qv_bias, "proj_weight": proj_weight, "proj_bias": proj_bias, "mlp_in_weight": mlp_in_weight, "mlp_in_bias": mlp_in_bias, "mlp_out_weight": mlp_out_weight, "mlp_out_bias": mlp_out_bias}


EPS = 1e-06
GELU_C = math.sqrt(2.0 / math.pi)

def layer_norm(inputs):
    center = inputs - lax.optimization_barrier(jnp.mean(inputs, axis=-1, keepdims=True))
    inverse = lax.rsqrt(lax.optimization_barrier(jnp.mean(center * center, axis=-1, keepdims=True)) + EPS)
    return (center * inverse, inverse)

def norm_back(upstream, normed, inverse):
    return inverse * (upstream - lax.optimization_barrier(jnp.mean(upstream, axis=-1, keepdims=True)) - normed * lax.optimization_barrier(jnp.mean(upstream * normed, axis=-1, keepdims=True)))

def gelu_pair(inputs):
    tangent = jnp.tanh(GELU_C * (inputs + 0.044715 * inputs * inputs * inputs))
    value = 0.5 * inputs * (1.0 + tangent)
    slope = 0.5 * (1.0 + tangent) + 0.5 * inputs * (1.0 - tangent * tangent) * GELU_C * (1.0 + 3.0 * 0.044715 * inputs * inputs)
    return (value, slope)

def matmul(left, right):
    return jnp.dot(left, right, preferred_element_type=jnp.float32)

def latent_block(latents, cotangent, modulation, weights):
    qkv_full, proj_full, in_full, out_full, qv_full, proj_bias_full, in_bias_full, out_bias_full = weights
    groups, length, width = latents.shape
    tokens = groups * length
    head_size = width // HEADS
    factor = head_size ** (-0.5)
    shift_attn, scale_attn, gate_attn, shift_mlp, scale_mlp, gate_mlp = [piece[:, None, :] for piece in jnp.split(modulation, 6, axis=1)]
    resid = latents.astype(jnp.float32)
    normed_attn, inverse_attn = layer_norm(resid)
    act_attn = (normed_attn * (1.0 + scale_attn) + shift_attn).astype(jnp.bfloat16).reshape(tokens, width)
    projected = matmul(act_attn, qkv_full)
    qv_float = qv_full.astype(jnp.float32)
    queries = (projected[:, :width] + qv_float[:width]).astype(jnp.bfloat16).reshape(groups, length, HEADS, head_size)
    keys = projected[:, width:2 * width].astype(jnp.bfloat16).reshape(groups, length, HEADS, head_size)
    values = (projected[:, 2 * width:] + qv_float[width:]).astype(jnp.bfloat16).reshape(groups, length, HEADS, head_size)
    queries_f = queries.astype(jnp.float32)
    keys_f = keys.astype(jnp.float32)
    values_f = values.astype(jnp.float32)
    scores = jnp.einsum('bqhd,bkhd->bhqk', queries_f, keys_f) * factor
    top = lax.optimization_barrier(jnp.max(scores, axis=-1, keepdims=True))
    log_total = top + jnp.log(lax.optimization_barrier(jnp.sum(jnp.exp(scores - top), axis=-1, keepdims=True)))
    probs = jnp.exp(scores - log_total).astype(jnp.bfloat16)
    attended = jnp.einsum('bhqk,bkhd->bqhd', probs.astype(jnp.float32), values_f).astype(jnp.bfloat16).reshape(tokens, width)
    attn_branch = (matmul(attended, proj_full) + proj_bias_full.astype(jnp.float32)).reshape(groups, length, width)
    mid = resid + gate_attn * attn_branch
    normed_mlp, inverse_mlp = layer_norm(mid)
    act_mlp = (normed_mlp * (1.0 + scale_mlp) + shift_mlp).astype(jnp.bfloat16).reshape(tokens, width)
    pre_gelu = matmul(act_mlp, in_full) + in_bias_full.astype(jnp.float32)
    gelu_value, gelu_slope = gelu_pair(pre_gelu)
    gelu_out = gelu_value.astype(jnp.bfloat16)
    mlp_branch = (matmul(gelu_out, out_full) + out_bias_full.astype(jnp.float32)).reshape(groups, length, width)
    block_out = mid + gate_mlp * mlp_branch
    cot = cotangent.astype(jnp.float32)
    grad_gate_mlp = lax.optimization_barrier(jnp.sum(cot * mlp_branch, axis=1))
    grad_mlp = (cot * gate_mlp).reshape(tokens, width)
    grad_mlp_b = grad_mlp.astype(jnp.bfloat16)
    grad_out_weight = matmul(gelu_out.T, grad_mlp_b)
    grad_out_bias = lax.optimization_barrier(jnp.sum(grad_mlp, axis=0))
    grad_pre = matmul(grad_mlp_b, out_full.T) * gelu_slope
    grad_pre_b = grad_pre.astype(jnp.bfloat16)
    grad_in_weight = matmul(act_mlp.T, grad_pre_b)
    grad_in_bias = lax.optimization_barrier(jnp.sum(grad_pre, axis=0))
    grad_act_mlp = matmul(grad_pre_b, in_full.T).reshape(groups, length, width)
    grad_shift_mlp = lax.optimization_barrier(jnp.sum(grad_act_mlp, axis=1))
    grad_scale_mlp = lax.optimization_barrier(jnp.sum(grad_act_mlp * normed_mlp, axis=1))
    grad_mid = cot + norm_back(grad_act_mlp * (1.0 + scale_mlp), normed_mlp, inverse_mlp)
    grad_gate_attn = lax.optimization_barrier(jnp.sum(grad_mid * attn_branch, axis=1))
    grad_attn = (grad_mid * gate_attn).reshape(tokens, width)
    grad_attn_b = grad_attn.astype(jnp.bfloat16)
    grad_proj_weight = matmul(attended.T, grad_attn_b)
    grad_proj_bias = lax.optimization_barrier(jnp.sum(grad_attn, axis=0))
    grad_attended = matmul(grad_attn_b, proj_full.T).astype(jnp.bfloat16).reshape(groups, length, HEADS, head_size)
    grad_attended_f = grad_attended.astype(jnp.float32)
    again = jnp.einsum('bqhd,bkhd->bhqk', queries_f, keys_f) * factor
    weights_exact = jnp.exp(again - log_total)
    weights_b = weights_exact.astype(jnp.bfloat16).astype(jnp.float32)
    grad_values = jnp.einsum('bhqk,bqhd->bkhd', weights_b, grad_attended_f)
    grad_probs = jnp.einsum('bqhd,bkhd->bhqk', grad_attended_f, values_f)
    inner = lax.optimization_barrier(jnp.sum(weights_exact * grad_probs, axis=-1, keepdims=True))
    grad_scores = (weights_exact * (grad_probs - inner) * factor).astype(jnp.bfloat16).astype(jnp.float32)
    grad_queries = jnp.einsum('bhqk,bkhd->bqhd', grad_scores, keys_f).reshape(tokens, width)
    grad_keys = jnp.einsum('bhqk,bqhd->bkhd', grad_scores, queries_f).reshape(tokens, width)
    grad_values = grad_values.reshape(tokens, width)
    grad_qkv_b = jnp.concatenate([grad_queries, grad_keys, grad_values], axis=1).astype(jnp.bfloat16)
    grad_qkv_weight = matmul(act_attn.T, grad_qkv_b)
    grad_qv_bias = jnp.concatenate([lax.optimization_barrier(jnp.sum(grad_queries, axis=0)), lax.optimization_barrier(jnp.sum(grad_values, axis=0))])
    grad_act_attn = matmul(grad_qkv_b, qkv_full.T).reshape(groups, length, width)
    grad_shift_attn = lax.optimization_barrier(jnp.sum(grad_act_attn, axis=1))
    grad_scale_attn = lax.optimization_barrier(jnp.sum(grad_act_attn * normed_attn, axis=1))
    grad_latents = grad_mid + norm_back(grad_act_attn * (1.0 + scale_attn), normed_attn, inverse_attn)
    grad_modulation = jnp.concatenate([grad_shift_attn, grad_scale_attn, grad_gate_attn, grad_shift_mlp, grad_scale_mlp, grad_gate_mlp], axis=1)
    grads = (grad_qkv_weight, grad_proj_weight, grad_in_weight, grad_out_weight, grad_qv_bias, grad_proj_bias, grad_in_bias, grad_out_bias)
    return (block_out, grad_latents, grad_modulation, grads)

def reference(latents_in, conditioning, out_cotangent, modulation_weight, modulation_bias, qkv_weight, qv_bias, proj_weight, proj_bias, mlp_in_weight, mlp_in_bias, mlp_out_weight, mlp_out_bias):
    cond_float = conditioning.astype(jnp.float32)
    cond_act = jax.nn.silu(cond_float).astype(jnp.bfloat16)
    modulation = matmul(cond_act, modulation_weight) + modulation_bias.astype(jnp.float32)
    group = math.gcd(LATENTS, 4)
    count = LATENTS // group
    weights = (qkv_weight, proj_weight, mlp_in_weight, mlp_out_weight, qv_bias, proj_bias, mlp_in_bias, mlp_out_bias)
    starting = tuple((jnp.zeros(item.shape, jnp.float32) for item in weights))

    def visit(totals, items):
        latents, cotangent, mods = items
        block_out, grad_latents, grad_modulation, grads = latent_block(latents, cotangent, mods, weights)
        return (tuple((first + second for first, second in zip(totals, grads))), (block_out, grad_latents, grad_modulation))
    totals, (outputs, grad_inputs, grad_mods) = lax.scan(visit, starting, (latents_in.reshape(count, group, L, D), out_cotangent.reshape(count, group, L, D), modulation.reshape(count, group, 6 * D)))
    grad_modulation = grad_mods.reshape(LATENTS, 6 * D)
    grad_modulation_weight = jnp.dot(cond_act.astype(jnp.float32).T, grad_modulation, precision=lax.Precision.HIGHEST)
    grad_modulation_bias = lax.optimization_barrier(jnp.sum(grad_modulation, axis=0))
    sigma = jax.nn.sigmoid(cond_float)
    silu_slope = sigma * (1.0 + cond_float * (1.0 - sigma))
    grad_conditioning = jnp.dot(grad_modulation, modulation_weight.astype(jnp.float32).T, precision=lax.Precision.HIGHEST) * silu_slope
    return (outputs.reshape(LATENTS, L, D), grad_inputs.reshape(LATENTS, L, D), grad_conditioning, grad_modulation_weight, grad_modulation_bias, totals[0], totals[4], totals[1], totals[5], totals[2], totals[6], totals[3], totals[7])
```

```python
import math

import jax
import jax.numpy as jnp
from jax import lax
from jax.sharding import PartitionSpec as P

HEADS = 12


EPS = 1e-06
GELU_C = math.sqrt(2.0 / math.pi)


def layer_norm(inputs):
    center = inputs - jnp.mean(inputs, axis=-1, keepdims=True)
    inverse = lax.rsqrt(jnp.mean(center * center, axis=-1, keepdims=True) + EPS)
    return (center * inverse, inverse)


def norm_back(upstream, normed, inverse):
    return inverse * (
        upstream
        - jnp.mean(upstream, axis=-1, keepdims=True)
        - normed * jnp.mean(upstream * normed, axis=-1, keepdims=True)
    )


def gelu_pair(inputs):
    tangent = jnp.tanh(GELU_C * (inputs + 0.044715 * inputs * inputs * inputs))
    value = 0.5 * inputs * (1.0 + tangent)
    slope = 0.5 * (1.0 + tangent) + 0.5 * inputs * (1.0 - tangent * tangent) * GELU_C * (
        1.0 + 3.0 * 0.044715 * inputs * inputs
    )
    return (value, slope)


def matmul(left, right):
    return jnp.dot(left, right, preferred_element_type=jnp.float32)


def matmul_right_t(left, right):
    return lax.dot_general(
        left, right, (((1,), (1,)), ((), ())), preferred_element_type=jnp.float32
    )


def matmul_left_t(left, right):
    return lax.dot_general(
        left, right, (((0,), (0,)), ((), ())), preferred_element_type=jnp.float32
    )


def exact_right_t(left, right):
    return lax.dot_general(
        left,
        right,
        (((1,), (1,)), ((), ())),
        precision=lax.Precision.HIGHEST,
        preferred_element_type=jnp.float32,
    )


def exact_left_t(left, right):
    return lax.dot_general(
        left,
        right,
        (((0,), (0,)), ((), ())),
        precision=lax.Precision.HIGHEST,
        preferred_element_type=jnp.float32,
    )


def reduce_rows(grad):
    within = lax.psum_scatter(
        grad.astype(jnp.bfloat16), "dp", scatter_dimension=0, tiled=True
    )
    across = lax.psum_scatter(within, "seq", scatter_dimension=0, tiled=True)
    return across.astype(jnp.float32)


def local(
    latents_in,
    conditioning,
    out_cotangent,
    modulation_weight,
    modulation_bias,
    qkv_weight,
    qv_bias,
    proj_weight,
    proj_bias,
    mlp_in_weight,
    mlp_in_bias,
    mlp_out_weight,
    mlp_out_bias,
):
    lat_count, local_len, width = latents_in.shape
    head_size = width // HEADS
    factor = head_size ** (-0.5)
    tokens = lat_count * local_len
    axes = ("dp", "seq")
    parts = lax.axis_size("dp") * lax.axis_size("seq")
    owner = lax.axis_index("dp") * lax.axis_size("seq") + lax.axis_index("seq")
    mod_rows = modulation_weight.shape[0]
    cond_float = conditioning.astype(jnp.float32)
    cond_act = jax.nn.silu(cond_float).astype(jnp.bfloat16)
    cond_all = lax.all_gather(cond_act, "dp", axis=0, tiled=True)
    cond_own = lax.dynamic_slice_in_dim(cond_all, owner * mod_rows, mod_rows, axis=1)
    mod_part = lax.psum_scatter(
        matmul(cond_own, modulation_weight), "dp", scatter_dimension=0, tiled=True
    )
    biases = (qv_bias, proj_bias, mlp_in_bias, mlp_out_bias, modulation_bias)
    joined = lax.all_gather(jnp.concatenate(biases), axes, axis=0)
    bounds = [0]
    for bias in biases:
        bounds.append(bounds[-1] + bias.shape[0])
    qv_full, proj_bias_full, in_bias_full, out_bias_full, mod_bias_full = [
        joined[:, low:high].reshape(-1) for low, high in zip(bounds[:-1], bounds[1:])
    ]
    modulation = lax.psum(mod_part, "seq") + mod_bias_full.astype(jnp.float32)
    qkv_full, proj_full, in_full, out_full = (
        lax.all_gather(qkv_weight, axes, axis=0, tiled=True),
        lax.all_gather(proj_weight, axes, axis=0, tiled=True),
        lax.all_gather(mlp_in_weight, axes, axis=0, tiled=True),
        lax.all_gather(mlp_out_weight, axes, axis=0, tiled=True),
    )
    shift_attn, scale_attn, gate_attn, shift_mlp, scale_mlp, gate_mlp = [
        piece[:, None, :] for piece in jnp.split(modulation, 6, axis=1)
    ]
    resid = latents_in.astype(jnp.float32)
    normed_attn, inverse_attn = layer_norm(resid)
    act_attn = (
        (normed_attn * (1.0 + scale_attn) + shift_attn).astype(jnp.bfloat16).reshape(tokens, width)
    )
    projected = matmul(act_attn, qkv_full)
    qv_float = qv_full.astype(jnp.float32)
    queries = (
        (projected[:, :width] + qv_float[:width])
        .astype(jnp.bfloat16)
        .reshape(lat_count, local_len, HEADS, head_size)
    )
    keys_local = (
        projected[:, width : 2 * width].astype(jnp.bfloat16).reshape(lat_count, local_len, width)
    )
    values_local = (
        (projected[:, 2 * width :] + qv_float[width:])
        .astype(jnp.bfloat16)
        .reshape(lat_count, local_len, width)
    )
    keys_all, values_all = (
        lax.all_gather(keys_local, "seq", axis=1, tiled=True),
        lax.all_gather(values_local, "seq", axis=1, tiled=True),
    )
    keys_all = keys_all.reshape(lat_count, -1, HEADS, head_size)
    values_all = values_all.reshape(lat_count, -1, HEADS, head_size)
    scores = (
        jnp.einsum("bqhd,bkhd->bhqk", queries, keys_all, preferred_element_type=jnp.float32)
        * factor
    )
    top = jnp.max(scores, axis=-1, keepdims=True)
    log_total = top + jnp.log(jnp.sum(jnp.exp(scores - top), axis=-1, keepdims=True))
    probs = jnp.exp(scores - log_total).astype(jnp.bfloat16)
    attended = (
        jnp.einsum("bhqk,bkhd->bqhd", probs, values_all, preferred_element_type=jnp.float32)
        .astype(jnp.bfloat16)
        .reshape(tokens, width)
    )
    attn_branch = (matmul(attended, proj_full) + proj_bias_full.astype(jnp.float32)).reshape(
        lat_count, local_len, width
    )
    mid = resid + gate_attn * attn_branch
    normed_mlp, inverse_mlp = layer_norm(mid)
    act_mlp = (
        (normed_mlp * (1.0 + scale_mlp) + shift_mlp).astype(jnp.bfloat16).reshape(tokens, width)
    )
    pre_gelu = matmul(act_mlp, in_full) + in_bias_full.astype(jnp.float32)
    gelu_value, gelu_slope = gelu_pair(pre_gelu)
    gelu_out = gelu_value.astype(jnp.bfloat16)
    mlp_branch = (matmul(gelu_out, out_full) + out_bias_full.astype(jnp.float32)).reshape(
        lat_count, local_len, width
    )
    block_out = mid + gate_mlp * mlp_branch
    back_qkv, back_proj, back_in, back_out = (qkv_full, proj_full, in_full, out_full)
    cot = out_cotangent.astype(jnp.float32)
    grad_gate_mlp = jnp.sum(cot * mlp_branch, axis=1)
    grad_mlp = (cot * gate_mlp).reshape(tokens, width)
    grad_mlp_b = grad_mlp.astype(jnp.bfloat16)
    grad_out_weight = matmul_left_t(gelu_out, grad_mlp_b)
    grad_out_bias = jnp.sum(grad_mlp, axis=0)
    grad_pre = matmul_right_t(grad_mlp_b, back_out) * gelu_slope
    grad_pre_b = grad_pre.astype(jnp.bfloat16)
    grad_in_weight = matmul_left_t(act_mlp, grad_pre_b)
    grad_in_bias = jnp.sum(grad_pre, axis=0)
    grad_act_mlp = matmul_right_t(grad_pre_b, back_in).reshape(lat_count, local_len, width)
    grad_shift_mlp = jnp.sum(grad_act_mlp, axis=1)
    grad_scale_mlp = jnp.sum(grad_act_mlp * normed_mlp, axis=1)
    grad_mid = cot + norm_back(grad_act_mlp * (1.0 + scale_mlp), normed_mlp, inverse_mlp)
    grad_gate_attn = jnp.sum(grad_mid * attn_branch, axis=1)
    grad_attn = (grad_mid * gate_attn).reshape(tokens, width)
    grad_attn_b = grad_attn.astype(jnp.bfloat16)
    grad_proj_weight = matmul_left_t(attended, grad_attn_b)
    grad_proj_bias = jnp.sum(grad_attn, axis=0)
    grad_attended = (
        matmul_right_t(grad_attn_b, back_proj)
        .astype(jnp.bfloat16)
        .reshape(lat_count, local_len, HEADS, head_size)
    )
    recomputed = (
        jnp.einsum("bqhd,bkhd->bhqk", queries, keys_all, preferred_element_type=jnp.float32)
        * factor
    )
    weights_exact = jnp.exp(recomputed - log_total)
    grad_probs = jnp.einsum(
        "bqhd,bkhd->bhqk", grad_attended, values_all, preferred_element_type=jnp.float32
    )
    inner = jnp.sum(weights_exact * grad_probs, axis=-1, keepdims=True)
    grad_scores = (weights_exact * (grad_probs - inner) * factor).astype(jnp.bfloat16)
    grad_queries = jnp.einsum(
        "bhqk,bkhd->bqhd", grad_scores, keys_all, preferred_element_type=jnp.float32
    ).reshape(tokens, width)
    weights_b = weights_exact.astype(jnp.bfloat16)
    grad_values_all = jnp.einsum(
        "bhqk,bqhd->bkhd", weights_b, grad_attended, preferred_element_type=jnp.float32
    )
    grad_keys_all = jnp.einsum(
        "bhqk,bqhd->bkhd", grad_scores, queries, preferred_element_type=jnp.float32
    )
    grad_keys, grad_values = (
        lax.psum_scatter(
            grad_keys_all.reshape(lat_count, -1, width), "seq", scatter_dimension=1, tiled=True
        ),
        lax.psum_scatter(
            grad_values_all.reshape(lat_count, -1, width), "seq", scatter_dimension=1, tiled=True
        ),
    )
    grad_keys = grad_keys.reshape(tokens, width)
    grad_values = grad_values.reshape(tokens, width)
    grad_qkv_b = jnp.concatenate([grad_queries, grad_keys, grad_values], axis=1).astype(
        jnp.bfloat16
    )
    grad_qkv_weight = matmul_left_t(act_attn, grad_qkv_b)
    grad_qv_bias = jnp.concatenate([jnp.sum(grad_queries, axis=0), jnp.sum(grad_values, axis=0)])
    grad_act_attn = matmul_right_t(grad_qkv_b, back_qkv).reshape(lat_count, local_len, width)
    grad_shift_attn = jnp.sum(grad_act_attn, axis=1)
    grad_scale_attn = jnp.sum(grad_act_attn * normed_attn, axis=1)
    grad_latents = grad_mid + norm_back(
        grad_act_attn * (1.0 + scale_attn), normed_attn, inverse_attn
    )
    grad_mod_part = jnp.concatenate(
        [
            grad_shift_attn,
            grad_scale_attn,
            grad_gate_attn,
            grad_shift_mlp,
            grad_scale_mlp,
            grad_gate_mlp,
        ],
        axis=1,
    )
    grad_modulation = lax.psum(grad_mod_part, "seq")
    sigma = jax.nn.sigmoid(cond_float)
    silu_slope = sigma * (1.0 + cond_float * (1.0 - sigma))
    grad_mod_all = lax.all_gather(grad_modulation, "dp", axis=0, tiled=True)
    through_own = exact_right_t(grad_mod_all, modulation_weight.astype(jnp.float32))
    through_all = lax.all_gather(through_own, axes, axis=1, tiled=True)
    through = lax.dynamic_slice_in_dim(
        through_all, lax.axis_index("dp") * lat_count, lat_count, axis=0
    )
    grad_conditioning = through * silu_slope
    grad_modulation_weight = exact_left_t(cond_own.astype(jnp.float32), grad_mod_all)
    bias_rows = modulation_bias.shape[0]
    grad_modulation_bias = lax.dynamic_slice_in_dim(
        jnp.sum(grad_mod_all, axis=0), owner * bias_rows, bias_rows, axis=0
    )
    owned_out, owned_in, owned_proj, owned_qkv = (
        reduce_rows(grad_out_weight),
        reduce_rows(grad_in_weight),
        reduce_rows(grad_proj_weight),
        reduce_rows(grad_qkv_weight),
    )
    bias_grads = jnp.concatenate(
        [
            grad.reshape(parts, -1)
            for grad in (grad_qv_bias, grad_proj_bias, grad_in_bias, grad_out_bias)
        ],
        axis=1,
    )
    owned_biases = lax.psum_scatter(bias_grads, axes, scatter_dimension=0, tiled=True)[0]
    owned_qv, owned_proj_bias, owned_in_bias, owned_out_bias = [
        owned_biases[low:high] for low, high in zip(bounds[:4], bounds[1:5])
    ]
    return (
        block_out,
        grad_latents,
        grad_conditioning,
        grad_modulation_weight,
        grad_modulation_bias,
        owned_qkv,
        owned_qv,
        owned_proj,
        owned_proj_bias,
        owned_in,
        owned_in_bias,
        owned_out,
        owned_out_bias,
    )


def solution(mesh):
    placed = (
        P("dp", "seq", None),
        P("dp", None),
        P("dp", "seq", None),
        P(("dp", "seq"), None),
        P(("dp", "seq")),
        P(("dp", "seq"), None),
        P(("dp", "seq")),
        P(("dp", "seq"), None),
        P(("dp", "seq")),
        P(("dp", "seq"), None),
        P(("dp", "seq")),
        P(("dp", "seq"), None),
        P(("dp", "seq")),
    )
    return jax.shard_map(
        local,
        mesh=mesh,
        in_specs=placed,
        out_specs=(
            P("dp", "seq", None),
            P("dp", "seq", None),
            P("dp", None),
            P(("dp", "seq"), None),
            P(("dp", "seq")),
            P(("dp", "seq"), None),
            P(("dp", "seq")),
            P(("dp", "seq"), None),
            P(("dp", "seq")),
            P(("dp", "seq"), None),
            P(("dp", "seq")),
            P(("dp", "seq"), None),
            P(("dp", "seq")),
        ),
        check_vma=False,
    )
```
